128 devices in a mesh: dp: 2 (over z_hi), seq: 32 (over y, x, core), tensor: 2 (over z_lo).
Axes of the slice: x: 4, y: 4, z: 4 (z_hi: 2, z_lo: 2; z = z_hi * 2 + z_lo), core: 2. Of those that a mesh axis runs over, the one named last changes fastest.
Arguments:
- queries: bfloat16 [2, 16384, 4096], P('dp', 'seq', 'tensor'), may hold values from -6 to 6
- keys: bfloat16 [2, 16384, 4096], P('dp', 'seq', 'tensor'), may hold values from -6 to 6
- values: bfloat16 [2, 16384, 4096], P('dp', 'seq', 'tensor'), may hold values from -40 to 40
- grad_out: bfloat16 [2, 16384, 4096], P('dp', 'seq', 'tensor'), may hold values from -48 to 48
- doc_lengths: int32 [2, 16], P('dp'), may hold values from 1 to 9216, 16384 in all within a row
- gain: float32 [4096], P('tensor'), may hold values from 0.1 to 1.9
Outputs:
- layer_out: bfloat16 [2, 16384, 4096], P('dp', 'seq', 'tensor')
- grad_queries: bfloat16 [2, 16384, 4096], P('dp', 'seq', 'tensor')
- grad_keys: bfloat16 [2, 16384, 4096], P('dp', 'seq', 'tensor')
- grad_values: bfloat16 [2, 16384, 4096], P('dp', 'seq', 'tensor')
- grad_gain: float32 [4096], P('tensor')
The draws below stay inside these ranges and needn't reach their ends.
Inputs may be any that keep to these rules, and one draw needn't show every extreme that they name: `doc_lengths`: each row sums to 16384; in every sequence the longest document has exactly 9216 tokens.
All inputs are finite; a program needn't handle non-finite values.
Results may differ from the reference program's by a relative error of at most 0.0063.
Values may be sent and summed in bfloat16 or wider, within the bound.
No kernel may reach another device: no remote copies, remote signals or barrier semaphores. Data moves between devices by JAX's collectives and lax.ppermute only.
A program may use at most 128 MiB of HBM per device.

```python
import math
import jax
import jax.numpy as jnp
import numpy as np
from jax import lax

HEADS = 32
HD = 128
TOK_DEV = 512
WIDTH = 4096
SEQS = 2
LENGTH = 16384
DOCS = 16
MOST = 9216
N_SEQ = 32


def draw_values(key, part):
    first, second = jax.random.split(key, 2)
    heads = jnp.arange(HEADS, dtype=jnp.float32)
    jitter = jax.random.uniform(first, (HEADS,), dtype=jnp.float32)
    base = jnp.clip(jax.random.normal(second, (SEQS, LENGTH, HEADS, HD), dtype=jnp.float32), -4.0, 4.0)
    scale = 10.0 ** ((heads + jitter) / HEADS)
    return (base * scale[None, None, :, None]).reshape(SEQS, LENGTH, WIDTH).astype(jnp.bfloat16)


def draw_grad_out(key, part):
    first, second = jax.random.split(key, 2)
    place = jnp.arange(LENGTH, dtype=jnp.float32) / LENGTH
    rows = (3.0 ** place)[None, :] * jnp.exp(jax.random.uniform(first, (SEQS, LENGTH), dtype=jnp.float32, minval=0.0, maxval=1.386))
    base = jnp.clip(jax.random.normal(second, (SEQS, LENGTH, WIDTH), dtype=jnp.float32), -4.0, 4.0)
    return (base * rows[:, :, None]).astype(jnp.bfloat16)


def levels(stream_key, extent, shards, smallest, largest):
    level = 1.0
    for dim, parts in shards:
        heights = jax.random.uniform(jax.random.fold_in(jax.random.fold_in(stream_key, 6), dim), (parts,), jnp.float32, smallest / len(shards), largest / len(shards))
        level = level * jnp.repeat(jnp.exp(heights), extent[dim] // parts).reshape((-1,) + (1,) * (len(extent) - 1 - dim))
    return level


def length_profile(count, total, bound, slope):
    loads = [(1 << 20) // math.isqrt(grade ** slope) + 1 for grade in range(2, count + 1)]
    rest, counts = total - bound - (count - 1), [1] * (count - 1)
    while rest > 0:
        candidates = [i for i in range(count - 1) if counts[i] < bound]
        pool, left = sum([loads[i] for i in candidates]), rest
        for i in candidates:
            more = min(bound - counts[i], max(1, left * loads[i] // pool), rest)
            counts[i] = counts[i] + more
            rest = rest - more
    return np.array([bound] + counts)


def uneven(key, number_of, total, limit, skew):
    if number_of == 2:
        one = jax.random.randint(key, (), max(1, total - limit), min(limit, total - 1) + 1)
        return jnp.stack([one, total - one])
    sizes = jnp.asarray(length_profile(number_of, total, limit, skew), jnp.int32)
    twos = (number_of - 1) // 2
    donor, sink = sizes[1:1 + 2 * twos:2], sizes[2:2 + 2 * twos:2]
    slack = jnp.minimum(donor - 1, limit - sink)
    moved = jax.random.randint(jax.random.fold_in(key, 1), (twos,), 0, 1 << 20) % (slack + 1)
    sizes = sizes.at[1:1 + 2 * twos:2].set(donor - moved).at[2:2 + 2 * twos:2].set(sink + moved)
    return sizes[jax.random.permutation(jax.random.fold_in(key, 2), number_of)]


def scatter_about(rng, dims, width, bound, cuts=(), held_as=jnp.bfloat16):
    drawn = jax.random.normal(rng, dims, jnp.float32) * width
    if len(cuts) > 0:
        drawn = levels(rng, dims, cuts, -0.22, 0.18) * drawn
    return jnp.clip(drawn, min=-bound, max=bound).astype(held_as)


def setup_inputs(seed: int = 0) -> dict:
    key_list = jax.random.split(jax.random.key(seed), 7)
    queries = scatter_about(key_list[0], (SEQS, LENGTH, WIDTH), 1.0, 6.0, ((0, 2), (1, 32), (2, 2)))
    keys = scatter_about(key_list[1], (SEQS, LENGTH, WIDTH), 1.0, 6.0, ((0, 2), (1, 32), (2, 2)))
    values = draw_values(jax.random.fold_in(key_list[6], 71), 0)
    grad_out = draw_grad_out(jax.random.fold_in(key_list[6], 71), 0)
    doc_lengths = jax.vmap(lambda own: uneven(own, DOCS, LENGTH, MOST, 2))(jax.random.split(key_list[4], SEQS)).reshape((SEQS, DOCS)).astype(jnp.int32)
    gain = jnp.clip(1.0 + 0.18 * jax.random.normal(key_list[5], (WIDTH,), jnp.float32), 0.1, 1.9)
    return {"queries": queries, "keys": keys, "values": values, "grad_out": grad_out, "doc_lengths": doc_lengths, "gain": gain}


epsilon = 1e-05

def block_tables(lengths):
    starts = jnp.cumsum(lengths) - lengths
    position = jnp.arange(LENGTH, dtype=jnp.int32)
    document = lax.optimization_barrier(jnp.sum((starts[None, :] <= position[:, None]).astype(jnp.int32), axis=1)) - 1
    numbers = jnp.arange(N_SEQ, dtype=jnp.int32)
    begins = numbers * TOK_DEV
    continues = jnp.logical_not(jnp.any(starts[None, :] == begins[:, None], axis=1))
    grouped = document.reshape(N_SEQ, TOK_DEV)
    first_doc = grouped[:, 0]
    last_doc = grouped[:, -1]
    first_block = starts[first_doc] // TOK_DEV
    last_block = (starts[last_doc] + lengths[last_doc] - 1) // TOK_DEV
    weight_in = continues[:, None] & (numbers[None, :] >= first_block[:, None]) & (numbers[None, :] < numbers[:, None])
    weight_back = (numbers[None, :] > numbers[:, None]) & (numbers[None, :] <= last_block[:, None])
    first_mask = (grouped == first_doc[:, None]) & continues[:, None]
    last_mask = grouped == last_doc[:, None]
    return (grouped, weight_in, weight_back, first_mask, last_mask)

def causal_scores(left, right, document):
    count = document.shape[0]
    lower = jnp.arange(count)[:, None] >= jnp.arange(count)[None, :]
    same = lower & (document[:, None] == document[None, :])
    raw = jnp.einsum('thd,shd->hts', left.astype(jnp.float32), right.astype(jnp.float32))
    return jnp.where(same[None], raw, 0.0).astype(jnp.bfloat16)

def carry_sum(weights, states):
    total = jnp.einsum('bc,chde->bhde', weights.astype(jnp.float32), states.astype(jnp.float32), precision=lax.Precision.HIGHEST)
    return total.astype(jnp.bfloat16)

def one_sequence(queries, keys, values, grad_out, lengths, gain):
    grouped, weight_in, weight_back, first_mask, last_mask = block_tables(lengths)
    shape = (N_SEQ, TOK_DEV, HEADS, HD)
    query = queries.reshape(shape)
    key = keys.reshape(shape)
    value = values.reshape(shape)
    key_last = jnp.where(last_mask[:, :, None, None], key, 0)
    value_last = jnp.where(last_mask[:, :, None, None], value, 0)
    query_first = jnp.where(first_mask[:, :, None, None], query, 0)
    state = jnp.einsum('bthd,bthe->bhde', key_last.astype(jnp.float32), value.astype(jnp.float32)).astype(jnp.bfloat16)
    carry_in = carry_sum(weight_in, state)

    def forward_block(items):
        query_block, key_block, value_block, doc_block, first_block, carry_block = items
        scores = causal_scores(query_block, key_block, doc_block)
        local = jnp.einsum('hts,shd->thd', scores.astype(jnp.float32), value_block.astype(jnp.float32))
        return local + jnp.einsum('thd,hde->the', first_block.astype(jnp.float32), carry_block.astype(jnp.float32))
    attended = lax.map(forward_block, (query, key, value, grouped, query_first, carry_in)).reshape(LENGTH, WIDTH)
    mean_squares = lax.optimization_barrier(jnp.mean(attended * attended, axis=1))
    rscale = lax.rsqrt(mean_squares + epsilon)
    unit = attended * rscale[:, None]
    layer_out = (gain * unit).astype(jnp.bfloat16)
    upstream = grad_out.astype(jnp.float32)
    gain_term = lax.optimization_barrier(jnp.sum(upstream * unit, axis=0))
    scaled = upstream * gain
    inner = lax.optimization_barrier(jnp.mean(scaled * unit, axis=1))
    d_att = (rscale[:, None] * (scaled - unit * inner[:, None])).astype(jnp.bfloat16).reshape(shape)
    d_first = jnp.where(first_mask[:, :, None, None], d_att, 0)
    back_state = jnp.einsum('bthd,bthe->bhde', query_first.astype(jnp.float32), d_att.astype(jnp.float32)).astype(jnp.bfloat16)
    carry_back = carry_sum(weight_back, back_state)

    def backward_block(items):
        query_block, key_block, value_block, doc_block, grad_block, grad_first, carry_block, value_end, key_end, back_block = items
        scores = causal_scores(query_block, key_block, doc_block)
        d_scores = causal_scores(grad_block, value_block, doc_block)
        grad_query = jnp.einsum('hts,shd->thd', d_scores.astype(jnp.float32), key_block.astype(jnp.float32))
        grad_query = grad_query + jnp.einsum('the,hde->thd', grad_first.astype(jnp.float32), carry_block.astype(jnp.float32))
        grad_key = jnp.einsum('hts,thd->shd', d_scores.astype(jnp.float32), query_block.astype(jnp.float32))
        grad_key = grad_key + jnp.einsum('she,hde->shd', value_end.astype(jnp.float32), back_block.astype(jnp.float32))
        grad_value = jnp.einsum('hts,the->she', scores.astype(jnp.float32), grad_block.astype(jnp.float32))
        grad_value = grad_value + jnp.einsum('shd,hde->she', key_end.astype(jnp.float32), back_block.astype(jnp.float32))
        return (grad_query.astype(jnp.bfloat16), grad_key.astype(jnp.bfloat16), grad_value.astype(jnp.bfloat16))
    grad_query, grad_key, grad_value = lax.map(backward_block, (query, key, value, grouped, d_att, d_first, carry_in, value_last, key_last, carry_back))
    return (layer_out, grad_query.reshape(LENGTH, WIDTH), grad_key.reshape(LENGTH, WIDTH), grad_value.reshape(LENGTH, WIDTH), gain_term)

def reference(queries, keys, values, grad_out, doc_lengths, gain):
    results = [one_sequence(queries[member], keys[member], values[member], grad_out[member], doc_lengths[member], gain) for member in range(SEQS)]
    layer_out = jnp.stack([item[0] for item in results])
    grad_queries = jnp.stack([item[1] for item in results])
    grad_keys = jnp.stack([item[2] for item in results])
    grad_values = jnp.stack([item[3] for item in results])
    grad_gain = results[0][4]
    for item in results[1:]:
        grad_gain = grad_gain + item[4]
    return (layer_out, grad_queries, grad_keys, grad_values, grad_gain)
```

```python
import functools

import jax
import jax.numpy as jnp
from jax import lax
from jax.experimental import pallas as pl
from jax.experimental.pallas import tpu as pltpu
from jax.sharding import PartitionSpec as P

HEADS = 32
HD = 128
TOK = 512
HALF = 256
N_SEQ = 32
SLICE = 64
GG_ROWS = 32
GROUP = 4
EPS = 1e-05

F32 = jnp.float32
BF16 = jnp.bfloat16
NN = (((1,), (0,)), ((), ()))
NT = (((1,), (1,)), ((), ()))
TN = (((0,), (0,)), ((), ()))


def mm(a, b, dims):
    return lax.dot_general(a, b, dims, preferred_element_type=F32)


def local_starts(lens):
    begin = lax.axis_index("seq") * TOK
    total = -begin
    starts = []
    for d in range(lens.shape[1]):
        starts.append(total)
        total = total + lens[0, d]
    return starts


def first_end(starts):
    end = jnp.int32(TOK)
    fresh = jnp.int32(0)
    for s in reversed(starts):
        end = jnp.where(s > 0, s, end)
        fresh = jnp.where(s == 0, 1, fresh)
    end = jnp.minimum(end, TOK)
    return jnp.where(fresh == 1, 0, end)


def last_start(starts):
    begin = jnp.int32(0)
    for s in starts:
        begin = jnp.where(s <= TOK - 1, s, begin)
    return jnp.maximum(begin, 0)


def rows_before(limit):
    t = lax.broadcasted_iota(jnp.int32, (TOK, HD), 0)
    return jnp.where(t < limit, 1.0, 0.0).astype(BF16)


def rows_from(limit):
    t = lax.broadcasted_iota(jnp.int32, (TOK, HD), 0)
    return jnp.where(t >= limit, 1.0, 0.0).astype(BF16)


def keeps(lens):
    bits = jnp.int32(0)
    total = jnp.int32(0)
    for d in range(lens.shape[1]):
        bits = bits | lax.shift_left(jnp.int32(1), lax.shift_right_logical(total, 9))
        total = total + lens[0, d]
    return [
        (1 - (lax.shift_right_logical(bits, b) & 1)).astype(F32) for b in range(N_SEQ)
    ]


def cols(g):
    return slice(g * HD, (g + 1) * HD)


def state_kernel(lens, k, v, out, mask):
    @pl.when(pl.program_id(0) == 0)
    def _():
        mask[...] = rows_from(last_start(local_starts(lens)))

    for g in range(GROUP):
        kl = k[:, cols(g)] * mask[...]
        out[cols(g), :] = mm(kl, v[:, cols(g)], TN).astype(BF16)


def scan_kernel(lens, x, out):
    keep = keeps(lens)
    acc = jnp.zeros((SLICE, HD), F32)
    for b in range(N_SEQ):
        rows = slice(b * SLICE, (b + 1) * SLICE)
        out[rows, :] = acc.astype(BF16)
        acc = x[rows, :].astype(F32) + keep[b] * acc


def scan_back_kernel(lens, x, out, gg):
    keep = keeps(lens)
    acc = jnp.zeros((SLICE, HD), F32)
    step = SLICE + GG_ROWS
    for b in reversed(range(N_SEQ)):
        out[b * SLICE:(b + 1) * SLICE, :] = acc.astype(BF16)
        acc = x[b * step:b * step + SLICE, :].astype(F32) + keep[b] * acc
    high = jnp.zeros((GG_ROWS // 2, HD), F32)
    low = jnp.zeros((GG_ROWS // 2, HD), F32)
    for b in range(N_SEQ):
        base = b * step + SLICE
        high = high + x[base:base + GG_ROWS // 2, :].astype(F32)
        low = low + x[base + GG_ROWS // 2:base + GG_ROWS, :].astype(F32)
    gg[...] = high + low


def build_masks(lens, mask, mask_t):
    starts = local_starts(lens)
    t = lax.broadcasted_iota(jnp.int32, (TOK, HD), 0)
    lane = lax.broadcasted_iota(jnp.int32, (TOK, HD), 1)
    begin = jnp.zeros((TOK, HD), jnp.int32)
    for s in starts:
        begin = jnp.where(t >= s, jnp.maximum(s, 0), begin)
    end = jnp.full((TOK, HD), TOK, jnp.int32)
    for s in reversed(starts):
        end = jnp.where(s > t, jnp.minimum(s, TOK), end)
    for c in range(TOK // HD):
        s = lane + c * HD
        mask[:, cols(c)] = jnp.where((s <= t) & (s >= begin), 1.0, 0.0).astype(BF16)
        mask_t[:, cols(c)] = jnp.where((s >= t) & (s < end), 1.0, 0.0).astype(BF16)


def attend_head(q, k, v, mask, out, g):
    c = cols(g)
    for r in range(2):
        rows = slice(r * HALF, (r + 1) * HALF)
        wide = (r + 1) * HALF
        s = mm(q[rows, c], k[0:wide, c], NT).astype(BF16) * mask[rows, 0:wide]
        out[rows, c] = mm(s, v[0:wide, c], NN)


def attend_first_kernel(lens, q, k, v, out, mask, mask_t):
    @pl.when(pl.program_id(0) == 0)
    def _():
        build_masks(lens, mask, mask_t)

    for g in range(GROUP):
        attend_head(q, k, v, mask, out, g)


def attend_second_kernel(q, k, v, mask, unused, out):
    for g in range(GROUP):
        attend_head(q, k, v, mask, out, g)


def sums_kernel(lens, local, q, carry, up, gain, out, mask, squares, inners):
    i = pl.program_id(0)

    @pl.when(i == 0)
    def _():
        mask[...] = rows_before(first_end(local_starts(lens)))
        squares[...] = jnp.zeros((TOK, HD), F32)
        inners[...] = jnp.zeros((TOK, HD), F32)

    sq = squares[...]
    inn = inners[...]
    for g in range(GROUP):
        c = cols(g)
        att = local[:, c] + mm(q[:, c] * mask[...], carry[c, :], NN)
        sq = sq + att * att
        inn = inn + att * (up[:, c].astype(F32) * gain[:, c])
    squares[...] = sq
    inners[...] = inn

    @pl.when(i == pl.num_programs(0) - 1)
    def _():
        ones = jnp.ones((8, HD), F32)
        row = lax.broadcasted_iota(jnp.int32, (8, TOK), 0)
        one = lax.dot_general(ones, sq, NT, precision=lax.Precision.HIGHEST, preferred_element_type=F32)
        two = lax.dot_general(ones, inn, NT, precision=lax.Precision.HIGHEST, preferred_element_type=F32)
        out[...] = jnp.where(row == 0, one, two)


def norm_kernel(lens, mine, other, local, q, carry, up, gain,
                layer, d_att, send, mask, rscale, inner, gains):
    i = pl.program_id(0)

    @pl.when(i == 0)
    def _():
        mask[...] = rows_before(first_end(local_starts(lens)))
        both = jnp.transpose(mine[...] + other[...], (1, 0))
        scale = 1.0 / (HEADS * HD)
        rs = lax.rsqrt(jnp.broadcast_to(both[:, 0:1], (TOK, HD)) * scale + EPS)
        rscale[...] = rs
        inner[...] = rs * (jnp.broadcast_to(both[:, 1:2], (TOK, HD)) * scale)

    step = SLICE + GG_ROWS
    for g in range(GROUP):
        c = cols(g)
        qf = q[:, c] * mask[...]
        att = local[:, c] + mm(qf, carry[c, :], NN)
        unit = att * rscale[...]
        layer[:, c] = (gain[:, c] * unit).astype(BF16)
        upstream = up[:, c].astype(F32)
        gains[pl.ds(i * GROUP + g, 1), :] = jnp.sum(upstream * unit, axis=0, keepdims=True)
        da = (rscale[...] * (upstream * gain[:, c] - unit * inner[...])).astype(BF16)
        d_att[:, c] = da
        back = mm(qf, da, TN).astype(BF16)
        base = pl.multiple_of((i * GROUP + g) * (2 * step), 2 * step)
        send[pl.ds(base, SLICE), :] = back[0:SLICE, :]
        send[pl.ds(base + step, SLICE), :] = back[SLICE:HD, :]

    @pl.when(i == pl.num_programs(0) - 1)
    def _():
        total = gains[...]
        high = total.astype(BF16)
        low = (total - high.astype(F32)).astype(BF16)
        for b in range(N_SEQ):
            base = b * step + SLICE
            send[base:base + GG_ROWS // 2, :] = high
            send[base + GG_ROWS // 2:base + GG_ROWS, :] = low


def query_kernel(lens, d_att, k, v, carry, mask, out, first):
    @pl.when(pl.program_id(0) == 0)
    def _():
        first[...] = rows_before(first_end(local_starts(lens)))

    for g in range(GROUP):
        c = cols(g)
        for r in range(2):
            rows = slice(r * HALF, (r + 1) * HALF)
            wide = (r + 1) * HALF
            da = d_att[rows, c]
            ds = mm(da, v[0:wide, c], NT).astype(BF16) * mask[rows, 0:wide]
            gq = mm(ds, k[0:wide, c], NN) + mm(da * first[rows, :], carry[c, :], NT)
            out[rows, c] = gq.astype(BF16)


def local_kernel(q, k, v, d_att, mask_t, gk, gv):
    for g in range(GROUP):
        c = cols(g)
        for r in range(2):
            rows = slice(r * HALF, (r + 1) * HALF)
            at = slice(r * HALF, TOK)
            m = mask_t[rows, at]
            s = mm(k[rows, c], q[at, c], NT).astype(BF16) * m
            gv[rows, c] = mm(s, d_att[at, c], NN)
            ds = mm(v[rows, c], d_att[at, c], NT).astype(BF16) * m
            gk[rows, c] = mm(ds, q[at, c], NN)


def close_kernel(lens, gk_local, gv_local, k, v, carry, gg_mine, gg_other, gk, gv, gg, mask):
    @pl.when(pl.program_id(0) == 0)
    def _():
        mask[...] = rows_from(last_start(local_starts(lens)))
        gg[...] = gg_mine[...] + gg_other[...]

    for g in range(GROUP):
        c = cols(g)
        m = mask[...]
        gk[:, c] = (gk_local[:, c] + mm(v[:, c] * m, carry[c, :], NT)).astype(BF16)
        gv[:, c] = (gv_local[:, c] + mm(k[:, c] * m, carry[c, :], NN)).astype(BF16)


SMEM = pl.BlockSpec(memory_space=pltpu.SMEM)
VMEM_LIMIT = 40 * 1024 * 1024


def params():
    return pltpu.CompilerParams(dimension_semantics=("arbitrary",), vmem_limit_bytes=VMEM_LIMIT)


def tokens(first=0):
    return pl.BlockSpec((None, TOK, GROUP * HD), lambda i: (0, 0, i + first))


def flat(first=0):
    return pl.BlockSpec((TOK, GROUP * HD), lambda i: (0, i + first))


def whole(*shape):
    return pl.BlockSpec(shape, lambda i: (0,) * len(shape))


def head_rows():
    return pl.BlockSpec((GROUP * HD, HD), lambda i: (i, 0))


def gains_spec():
    return pl.BlockSpec((1, GROUP * HD), lambda i: (0, i))


def cost(flops, bytes_accessed):
    return pl.CostEstimate(flops=flops, transcendentals=0, bytes_accessed=bytes_accessed)


def struct(shape, dtype):
    return jax.ShapeDtypeStruct(shape, dtype)


def exchange(x, axis):
    return lax.ppermute(x, axis, [(0, 1), (1, 0)])


def swap(x):
    return lax.all_to_all(x, "seq", 0, 0, tiled=True)


def body(queries, keys, values, grad_out, doc_lengths, gain):
    width = queries.shape[2]
    heads = width // HD
    steps = heads // GROUP
    half = steps // 2
    gain = gain.reshape(1, width)
    lens = doc_lengths
    wide = struct((1, TOK, width), BF16)
    state_shape = (heads * HD, HD)
    column = lambda dtype: pltpu.VMEM((TOK, HD), dtype)
    mb = 1 << 20
    unit = 2 * heads * TOK * TOK * HD

    state = pl.pallas_call(
        state_kernel, grid=(steps,), name="state",
        in_specs=[SMEM, tokens(), tokens()], out_specs=head_rows(),
        out_shape=struct(state_shape, BF16), scratch_shapes=[column(BF16)],
        compiler_params=params(), cost_estimate=cost(unit // 4, 5 * mb),
    )(lens, keys, values)
    scattered = swap(state)
    local, mask, mask_t = pl.pallas_call(
        attend_first_kernel, grid=(half,), name="attend_first",
        in_specs=[SMEM, tokens(), tokens(), tokens()],
        out_specs=[flat(), whole(TOK, TOK), whole(TOK, TOK)],
        out_shape=[struct((TOK, width), F32), struct((TOK, TOK), BF16), struct((TOK, TOK), BF16)],
        compiler_params=params(), cost_estimate=cost(unit, 6 * mb),
    )(lens, queries, keys, values)
    summed = pl.pallas_call(
        scan_kernel, grid=(1,), name="scan",
        in_specs=[SMEM, whole(*state_shape)], out_specs=whole(*state_shape),
        out_shape=struct(state_shape, BF16),
        compiler_params=params(), cost_estimate=cost(mb, mb),
    )(lens, scattered)
    summed, local = lax.optimization_barrier((summed, local))
    carry_in = swap(summed)
    local = pl.pallas_call(
        attend_second_kernel, grid=(half,), name="attend_second",
        in_specs=[tokens(half), tokens(half), tokens(half), whole(TOK, TOK),
                  pl.BlockSpec(memory_space=pl.ANY)],
        out_specs=flat(half), out_shape=struct((TOK, width), F32),
        input_output_aliases={4: 0},
        compiler_params=params(), cost_estimate=cost(unit, 6 * mb),
    )(queries, keys, values, mask, local)
    sums = pl.pallas_call(
        sums_kernel, grid=(steps,), name="sums",
        in_specs=[SMEM, flat(), tokens(), head_rows(), tokens(), gains_spec()],
        out_specs=whole(8, TOK), out_shape=struct((8, TOK), F32),
        scratch_shapes=[column(BF16), column(F32), column(F32)],
        compiler_params=params(), cost_estimate=cost(unit // 4, 9 * mb),
    )(lens, local, queries, carry_in, grad_out, gain)
    other = exchange(sums, "tensor")
    step = SLICE + GG_ROWS
    send_shape = (N_SEQ * step, HD)
    layer_out, d_att, send = pl.pallas_call(
        norm_kernel, grid=(steps,), name="norm",
        in_specs=[SMEM, whole(8, TOK), whole(8, TOK), flat(), tokens(), head_rows(), tokens(),
                  gains_spec()],
        out_specs=[tokens(), flat(), whole(*send_shape)],
        out_shape=[wide, struct((TOK, width), BF16), struct(send_shape, BF16)],
        scratch_shapes=[column(BF16), column(F32), column(F32), pltpu.VMEM((heads, HD), F32)],
        compiler_params=params(), cost_estimate=cost(unit // 2, 13 * mb),
    )(lens, sums, other, local, queries, carry_in, grad_out, gain)
    back = swap(send)
    grad_queries = pl.pallas_call(
        query_kernel, grid=(steps,), name="grad_query",
        in_specs=[SMEM, flat(), tokens(), tokens(), head_rows(), whole(TOK, TOK)],
        out_specs=tokens(), out_shape=wide, scratch_shapes=[column(BF16)],
        compiler_params=params(), cost_estimate=cost(2 * unit, 9 * mb),
    )(lens, d_att, keys, values, carry_in, mask)
    back_sum, gg_mine = pl.pallas_call(
        scan_back_kernel, grid=(1,), name="scan_back",
        in_specs=[SMEM, whole(*send_shape)],
        out_specs=[whole(*state_shape), whole(GG_ROWS // 2, HD)],
        out_shape=[struct(state_shape, BF16), struct((GG_ROWS // 2, HD), F32)],
        compiler_params=params(), cost_estimate=cost(mb, mb),
    )(lens, back)
    back_sum, gg_mine, grad_queries, d_att = lax.optimization_barrier(
        (back_sum, gg_mine, grad_queries, d_att))
    carry_back = swap(back_sum)
    gg_other = exchange(gg_mine, "dp")
    gk_local, gv_local = pl.pallas_call(
        local_kernel, grid=(steps,), name="grad_local",
        in_specs=[tokens(), tokens(), tokens(), flat(), whole(TOK, TOK)],
        out_specs=[flat(), flat()],
        out_shape=[struct((TOK, width), F32), struct((TOK, width), F32)],
        compiler_params=params(), cost_estimate=cost(4 * unit, 16 * mb),
    )(queries, keys, values, d_att, mask_t)
    gg_shape = (GG_ROWS // 2, HD)
    grad_keys, grad_values, grad_gain = pl.pallas_call(
        close_kernel, grid=(steps,), name="grad_close",
        in_specs=[SMEM, flat(), flat(), tokens(), tokens(), head_rows(), whole(*gg_shape),
                  whole(*gg_shape)],
        out_specs=[tokens(), tokens(), whole(*gg_shape)],
        out_shape=[wide, wide, struct(gg_shape, F32)], scratch_shapes=[column(BF16)],
        compiler_params=params(), cost_estimate=cost(unit // 2, 17 * mb),
    )(lens, gk_local, gv_local, keys, values, carry_back, gg_mine, gg_other)
    return layer_out, grad_queries, grad_keys, grad_values, grad_gain.reshape(width)


def solution(mesh):
    spread = P("dp", "seq", "tensor")
    return jax.shard_map(
        body, mesh=mesh,
        in_specs=(spread, spread, spread, spread, P("dp", None), P("tensor")),
        out_specs=(spread, spread, spread, spread, P("tensor")),
        check_vma=False,
    )
```

```python
import jax
import jax.numpy as jnp
from jax import lax
from jax.experimental import pallas as pl
from jax.experimental.pallas import tpu as pltpu
from jax.sharding import PartitionSpec as P

HEADS = 32
HD = 128
TOK = 512
HALF = 256
N_SEQ = 32
SLICE = 64
GG_ROWS = 32
GROUP = 2
EPS = 1e-05
BACK_SPLIT = 10

F32 = jnp.float32
BF16 = jnp.bfloat16
LOCAL = BF16
NN = (((1,), (0,)), ((), ()))
NT = (((1,), (1,)), ((), ()))
TN = (((0,), (0,)), ((), ()))
HALVES = (slice(0, HALF), slice(HALF, TOK))


def mm(a, b, dims):
    return lax.dot_general(a, b, dims, preferred_element_type=F32)


def cols(g):
    return slice(g * HD, (g + 1) * HD)


def local_starts(lens):
    total = -(lax.axis_index("seq") * TOK)
    starts = []
    for d in range(lens.shape[1]):
        starts.append(total)
        total = total + lens[0, d]
    return starts


def front_end(starts, begin, end):
    stop = jnp.int32(end)
    fresh = jnp.int32(0)
    for s in reversed(starts):
        stop = jnp.where(s > begin, s, stop)
        fresh = jnp.where(s == begin, 1, fresh)
    return jnp.where(fresh == 1, begin, jnp.minimum(stop, end))


def tail_start(starts, begin, end):
    start = jnp.int32(begin)
    for s in starts:
        start = jnp.where(s < end, s, start)
    return jnp.maximum(start, begin)


def keep_of(starts, begin, end):
    hit = jnp.int32(0)
    for s in starts:
        hit = jnp.where((s >= begin) & (s < end), 1, hit)
    return (1 - hit).astype(F32)


def front_mask(starts):
    t = lax.broadcasted_iota(jnp.int32, (TOK, HD), 0)
    limit = jnp.where(t < HALF, front_end(starts, 0, HALF), front_end(starts, HALF, TOK))
    return jnp.where(t < limit, 1.0, 0.0).astype(BF16)


def tail_mask(starts):
    t = lax.broadcasted_iota(jnp.int32, (TOK, HD), 0)
    limit = jnp.where(t < HALF, tail_start(starts, 0, HALF), tail_start(starts, HALF, TOK))
    return jnp.where(t >= limit, 1.0, 0.0).astype(BF16)


def keeps(lens):
    bits = jnp.int32(0)
    total = jnp.int32(0)
    for d in range(lens.shape[1]):
        bits = bits | lax.shift_left(jnp.int32(1), lax.shift_right_logical(total, 9))
        total = total + lens[0, d]
    return [(1 - (lax.shift_right_logical(bits, b) & 1)).astype(F32) for b in range(N_SEQ)]


def build_masks(starts, mask, mask_t):
    t = lax.broadcasted_iota(jnp.int32, (TOK, HD), 0)
    lane = lax.broadcasted_iota(jnp.int32, (TOK, HD), 1)
    base = jnp.where(t < HALF, lane, lane + HALF)
    begin = jnp.zeros((TOK, HD), jnp.int32)
    for s in starts:
        begin = jnp.where(t >= s, jnp.maximum(s, 0), begin)
    end = jnp.full((TOK, HD), TOK, jnp.int32)
    for s in reversed(starts):
        end = jnp.where(s > t, jnp.minimum(s, TOK), end)
    for c in range(HALF // HD):
        s = base + c * HD
        mask[:, cols(c)] = jnp.where((s <= t) & (s >= begin), 1.0, 0.0).astype(BF16)
        mask_t[:, cols(c)] = jnp.where((s >= t) & (s < end), 1.0, 0.0).astype(BF16)


def second_carry(own, keep, earlier):
    return (own.astype(F32) + keep * earlier.astype(F32)).astype(BF16)


def token_cols(ref, h):
    return ref.at[0, :, pl.ds(h * HD if isinstance(h, int) else pl.multiple_of(h * HD, HD), HD)]


def head_rows(ref, h):
    return ref.at[pl.ds(h * HD if isinstance(h, int) else pl.multiple_of(h * HD, HD), HD), :]


def chunk(ref, h):
    return ref.at[h]


class Stream:
    def __init__(self, hbm, view, buf, sem, first=0, out=False):
        self.hbm, self.view, self.buf, self.sem, self.first, self.out = hbm, view, buf, sem, first, out

    def copy(self, i):
        far, near = self.view(self.hbm, i + self.first), self.buf.at[i]
        src, dst = (near, far) if self.out else (far, near)
        return pltpu.make_async_copy(src, dst, self.sem.at[i])

    def start(self, i):
        self.copy(i).start()

    def wait(self, i):
        self.copy(i).wait()


def start_all(n, streams):
    for i in range(n):
        for s in streams:
            s.start(i)


def loop(n, ins, outs, step, group=GROUP):
    def one(j, carry):
        for g in range(group):
            for s in ins:
                s.wait(j * group + g)
        for g in range(group):
            step(j * group + g)
        for g in range(group):
            for s in outs:
                s.start(j * group + g)
        return carry

    lax.fori_loop(0, n // group, one, 0)
    for i in range(n):
        for s in outs:
            s.wait(i)


def state_kernel(lens, k, v, out, early, k_buf, v_buf, o_buf, e_buf, mask, lens_s, lens_sem, sems):
    n = k_buf.shape[0]
    ahead = pltpu.make_async_copy(lens, lens_s, lens_sem)
    ahead.start()
    ins = [Stream(k, token_cols, k_buf, sems.at[0]), Stream(v, token_cols, v_buf, sems.at[1])]
    start_all(n, ins)
    ahead.wait()
    starts = local_starts(lens_s)
    mask[...] = tail_mask(starts)
    keep = keep_of(starts, HALF, TOK)

    def step(i):
        a, b = (mm(k_buf[i, r, :] * mask[r, :], v_buf[i, r, :], TN) for r in HALVES)
        e_buf[i] = a.astype(BF16)
        o_buf[i] = (b + keep * a).astype(BF16)

    loop(n, ins, [Stream(out, head_rows, o_buf, sems.at[2], out=True),
                  Stream(early, head_rows, e_buf, sems.at[3], out=True)], step)


def scan_kernel(lens, x, out, x_buf, o_buf, lens_s, lens_sem, sems):
    n = x_buf.shape[0]
    rows = x_buf.shape[2]
    view = lambda ref, i: ref.at[:, pl.ds(i * rows, rows), :]
    ahead = pltpu.make_async_copy(lens, lens_s, lens_sem)
    ahead.start()
    ins = [Stream(x, view, x_buf, sems.at[0])]
    start_all(n, ins)
    ahead.wait()
    keep = keeps(lens_s)

    def step(i):
        acc = jnp.zeros((rows, HD), F32)
        for b in range(N_SEQ):
            o_buf[i, b] = acc.astype(BF16)
            acc = x_buf[i, b].astype(F32) + keep[b] * acc

    loop(n, ins, [Stream(out, view, o_buf, sems.at[1], out=True)], step, group=1)


def scan_back_kernel(lens, x, out, gg, x_buf, o_buf, g_buf, lens_s, lens_sem, sems):
    n = x_buf.shape[0]
    rows = x_buf.shape[2]
    view = lambda ref, i: ref.at[:, pl.ds(i * rows, rows), :]
    ahead = pltpu.make_async_copy(lens, lens_s, lens_sem)
    ahead.start()
    ins = [Stream(x, view, x_buf, sems.at[0])]
    start_all(n, ins)
    gains = pltpu.make_async_copy(x.at[:, pl.ds(SLICE, GG_ROWS), :], g_buf, sems.at[2, 0])
    gains.start()
    ahead.wait()
    keep = keeps(lens_s)

    def step(i):
        acc = jnp.zeros((rows, HD), F32)
        for b in reversed(range(N_SEQ)):
            o_buf[i, b] = acc.astype(BF16)
            acc = x_buf[i, b].astype(F32) + keep[b] * acc

    loop(n, ins, [Stream(out, view, o_buf, sems.at[1], out=True)], step, group=1)
    gains.wait()
    half = GG_ROWS // 2
    total = jnp.zeros((half, HD), F32)
    for b in range(N_SEQ):
        total = total + (g_buf[b, 0:half, :].astype(F32) + g_buf[b, half:GG_ROWS, :].astype(F32))
    gg[...] = total


def attend_head(q, k, v, mask, out, i):
    for r in HALVES:
        s = mm(q[i, r, :], k[i, r, :], NT).astype(BF16) * mask[r, :]
        out[i, r, :] = mm(s, v[i, r, :], NN).astype(LOCAL)


def attend_first_kernel(lens, q, k, v, out, mask_out, mask_t_out, q_buf, k_buf, v_buf, o_buf,
                        mask, mask_t, lens_s, lens_sem, mask_sem, sems):
    n = q_buf.shape[0]
    ahead = pltpu.make_async_copy(lens, lens_s, lens_sem)
    ahead.start()
    ins = [Stream(ref, token_cols, buf, sems.at[j])
           for j, (ref, buf) in enumerate(((q, q_buf), (k, k_buf), (v, v_buf)))]
    start_all(n, ins)
    ahead.wait()
    build_masks(local_starts(lens_s), mask, mask_t)
    one = pltpu.make_async_copy(mask, mask_out, mask_sem.at[0])
    two = pltpu.make_async_copy(mask_t, mask_t_out, mask_sem.at[1])
    one.start()
    two.start()
    loop(n, ins, [Stream(out, chunk, o_buf, sems.at[3], out=True)],
         lambda i: attend_head(q_buf, k_buf, v_buf, mask, o_buf, i))
    one.wait()
    two.wait()


def attend_second_kernel(q, k, v, mask_in, unused, out, q_buf, k_buf, v_buf, o_buf,
                         mask, mask_sem, sems):
    n = q_buf.shape[0]
    first = out.shape[0] - n
    ahead = pltpu.make_async_copy(mask_in, mask, mask_sem)
    ahead.start()
    ins = [Stream(ref, token_cols, buf, sems.at[j], first=first)
           for j, (ref, buf) in enumerate(((q, q_buf), (k, k_buf), (v, v_buf)))]
    start_all(n, ins)
    ahead.wait()
    loop(n, ins, [Stream(out, chunk, o_buf, sems.at[3], first=first, out=True)],
         lambda i: attend_head(q_buf, k_buf, v_buf, mask, o_buf, i))


def sums_kernel(lens, local, q, carry, early, up, gain, out, local_buf, q_buf, carry_buf, early_buf,
                up_buf, gain_buf, mask, squares, inners, lens_s, lens_sem, sems):
    n = q_buf.shape[0]
    ahead = pltpu.make_async_copy(lens, lens_s, lens_sem)
    ahead.start()
    scales = pltpu.make_async_copy(gain, gain_buf, sems.at[5, 0])
    scales.start()
    ins = [Stream(local, chunk, local_buf, sems.at[0]),
           Stream(q, token_cols, q_buf, sems.at[1]),
           Stream(carry, head_rows, carry_buf, sems.at[2]),
           Stream(early, head_rows, early_buf, sems.at[3]),
           Stream(up, token_cols, up_buf, sems.at[4])]
    start_all(n, ins)
    ahead.wait()
    starts = local_starts(lens_s)
    mask[...] = front_mask(starts)
    keep = keep_of(starts, 0, HALF)
    squares[...] = jnp.zeros((TOK, HD), F32)
    inners[...] = jnp.zeros((TOK, HD), F32)
    scales.wait()

    def step(i):
        carries = (carry_buf[i], second_carry(early_buf[i], keep, carry_buf[i]))
        for r, c in zip(HALVES, carries):
            a = local_buf[i, r, :].astype(F32) + mm(q_buf[i, r, :] * mask[r, :], c, NN)
            squares[r, :] = squares[r, :] + a * a
            inners[r, :] = inners[r, :] + a * (up_buf[i, r, :].astype(F32) * gain_buf[i])

    loop(n, ins, [], step)
    ones = jnp.ones((8, HD), F32)
    row = lax.broadcasted_iota(jnp.int32, (8, TOK), 0)
    exact = dict(precision=lax.Precision.HIGHEST, preferred_element_type=F32)
    one = lax.dot_general(ones, squares[...], NT, **exact)
    two = lax.dot_general(ones, inners[...], NT, **exact)
    out[...] = jnp.where(row == 0, one, two)


def norm_kernel(lens, mine, other, local, q, carry, early, up, gain, layer, d_att, send, late,
                local_buf, q_buf, carry_buf, early_buf, up_buf, layer_buf, d_buf, send_buf, late_buf, mask, rscale, inner, gains,
                lens_s, lens_sem, sems):
    n = q_buf.shape[0]
    ahead = pltpu.make_async_copy(lens, lens_s, lens_sem)
    ahead.start()
    ins = [Stream(local, chunk, local_buf, sems.at[0]),
           Stream(q, token_cols, q_buf, sems.at[1]),
           Stream(carry, head_rows, carry_buf, sems.at[2]),
           Stream(early, head_rows, early_buf, sems.at[3]),
           Stream(up, token_cols, up_buf, sems.at[4])]
    start_all(n, ins)
    both = jnp.transpose(mine[...] + other[...], (1, 0))
    scale = 1.0 / (HEADS * HD)
    rs = lax.rsqrt(jnp.broadcast_to(both[:, 0:1], (TOK, HD)) * scale + EPS)
    rscale[...] = rs
    inner[...] = rs * (jnp.broadcast_to(both[:, 1:2], (TOK, HD)) * scale)
    ahead.wait()
    starts = local_starts(lens_s)
    mask[...] = front_mask(starts)
    keep = keep_of(starts, 0, HALF)

    def step(i):
        gg = gain[i]
        total = jnp.zeros((1, HD), F32)
        backs = []
        carries = (carry_buf[i], second_carry(early_buf[i], keep, carry_buf[i]))
        for r, c in zip(HALVES, carries):
            rs = rscale[r, :]
            front = q_buf[i, r, :] * mask[r, :]
            unit = (local_buf[i, r, :].astype(F32) + mm(front, c, NN)) * rs
            layer_buf[i, r, :] = (gg * unit).astype(BF16)
            upstream = up_buf[i, r, :].astype(F32)
            total = total + jnp.sum(upstream * unit, axis=0, keepdims=True)
            da = (rs * (upstream * gg - unit * inner[r, :])).astype(BF16)
            d_buf[i, r, :] = da
            backs.append(mm(front, da, TN))
        gains[pl.ds(i, 1), :] = total
        late_buf[i] = backs[1].astype(BF16)
        back = (backs[0] + keep * backs[1]).astype(BF16)
        send_buf[2 * i, 0:SLICE, :] = back[0:SLICE, :]
        send_buf[2 * i + 1, 0:SLICE, :] = back[SLICE:HD, :]

    loop(n, ins, [Stream(layer, token_cols, layer_buf, sems.at[5], out=True),
                  Stream(d_att, chunk, d_buf, sems.at[6], out=True),
                  Stream(late, head_rows, late_buf, sems.at[7], out=True)], step)
    total = gains[...]
    high = total.astype(BF16)
    low = (total - high.astype(F32)).astype(BF16)
    half = GG_ROWS // 2
    for b in range(N_SEQ):
        send_buf[b, SLICE:SLICE + half, :] = high
        send_buf[b, SLICE + half:SLICE + GG_ROWS, :] = low
    last = pltpu.make_async_copy(send_buf, send, lens_sem)
    last.start()
    last.wait()


def grad_kernel(first, lens, d_att, q, k, v, carry, early, mask_in, mask_t_in, gq, gk, gv,
                d_buf, q_buf, k_buf, v_buf, c_buf, e_buf, gq_buf, gk_buf, gv_buf,
                mask, mask_t, front, lens_s, lens_sem, mask_sem, sems):
    n = q_buf.shape[0]
    ahead = pltpu.make_async_copy(lens, lens_s, lens_sem)
    ahead.start()
    one = pltpu.make_async_copy(mask_in, mask, mask_sem.at[0])
    two = pltpu.make_async_copy(mask_t_in, mask_t, mask_sem.at[1])
    one.start()
    two.start()
    ins = [Stream(d_att, chunk, d_buf, sems.at[0], first=first),
           Stream(q, token_cols, q_buf, sems.at[1], first=first),
           Stream(k, token_cols, k_buf, sems.at[2], first=first),
           Stream(v, token_cols, v_buf, sems.at[3], first=first),
           Stream(carry, head_rows, c_buf, sems.at[4], first=first),
           Stream(early, head_rows, e_buf, sems.at[5], first=first)]
    start_all(n, ins)
    ahead.wait()
    starts = local_starts(lens_s)
    front[...] = front_mask(starts)
    keep = keep_of(starts, 0, HALF)
    one.wait()
    two.wait()

    def step(i):
        carries = (c_buf[i], second_carry(e_buf[i], keep, c_buf[i]))
        for r, c in zip(HALVES, carries):
            da, qr, kr, vr = d_buf[i, r, :], q_buf[i, r, :], k_buf[i, r, :], v_buf[i, r, :]
            ds = mm(da, vr, NT).astype(BF16) * mask[r, :]
            gq_buf[i, r, :] = (mm(ds, kr, NN) + mm(da * front[r, :], c, NT)).astype(BF16)
            s = mm(kr, qr, NT).astype(BF16) * mask_t[r, :]
            gv_buf[i, r, :] = mm(s, da, NN).astype(LOCAL)
            ds = mm(vr, da, NT).astype(BF16) * mask_t[r, :]
            gk_buf[i, r, :] = mm(ds, qr, NN).astype(LOCAL)

    outs = [Stream(gq, token_cols, gq_buf, sems.at[6], first=first, out=True),
            Stream(gk, chunk, gk_buf, sems.at[7], first=first, out=True),
            Stream(gv, chunk, gv_buf, sems.at[8], first=first, out=True)]
    loop(n, ins, outs, step)


def close_kernel(lens, gk_local, gv_local, k, v, carry, late, gg_mine, gg_other, gk, gv, gg,
                 gk_buf, gv_buf, k_buf, v_buf, c_buf, l_buf, gk_out, gv_out, mask, lens_s, lens_sem, sems):
    n = k_buf.shape[0]
    ahead = pltpu.make_async_copy(lens, lens_s, lens_sem)
    ahead.start()
    ins = [Stream(gk_local, chunk, gk_buf, sems.at[0]),
           Stream(gv_local, chunk, gv_buf, sems.at[1]),
           Stream(k, token_cols, k_buf, sems.at[2]),
           Stream(v, token_cols, v_buf, sems.at[3]),
           Stream(carry, head_rows, c_buf, sems.at[4]),
           Stream(late, head_rows, l_buf, sems.at[5])]
    start_all(n, ins)
    gg[...] = gg_mine[...] + gg_other[...]
    ahead.wait()
    starts = local_starts(lens_s)
    mask[...] = tail_mask(starts)
    keep = keep_of(starts, HALF, TOK)

    def step(i):
        carries = (second_carry(l_buf[i], keep, c_buf[i]), c_buf[i])
        for r, c in zip(HALVES, carries):
            m = mask[r, :]
            gk_out[i, r, :] = (gk_buf[i, r, :].astype(F32) + mm(v_buf[i, r, :] * m, c, NT)).astype(BF16)
            gv_out[i, r, :] = (gv_buf[i, r, :].astype(F32) + mm(k_buf[i, r, :] * m, c, NN)).astype(BF16)

    loop(n, ins, [Stream(gk, token_cols, gk_out, sems.at[6], out=True),
                  Stream(gv, token_cols, gv_out, sems.at[7], out=True)], step)


HBM = pl.BlockSpec(memory_space=pltpu.HBM)
ANY = pl.BlockSpec(memory_space=pl.ANY)
NEAR = pl.BlockSpec(memory_space=pltpu.VMEM)
MB = 1 << 20
FULL_GRANT = 60 * MB
PART_GRANT = 52 * MB
SMALL_GRANT = 8 * MB
SCALARS = [pltpu.SMEM((1, 16), jnp.int32), pltpu.SemaphoreType.DMA(())]


def struct(shape, dtype):
    return jax.ShapeDtypeStruct(shape, dtype)


def near(shape, dtype):
    return pltpu.VMEM(shape, dtype)


def call(kernel, name, ins, outs, out_shape, scratch, flops, traffic, grant=FULL_GRANT, alias=None):
    return pl.pallas_call(
        kernel, name=name, in_specs=ins, out_specs=outs, out_shape=out_shape,
        scratch_shapes=scratch, input_output_aliases=alias or {},
        compiler_params=pltpu.CompilerParams(vmem_limit_bytes=grant),
        cost_estimate=pl.CostEstimate(flops=flops, transcendentals=0, bytes_accessed=traffic))


def sems(*shape):
    return pltpu.SemaphoreType.DMA(shape)


def exchange(x, axis):
    return lax.ppermute(x, axis, [(0, 1), (1, 0)])


def swap(x):
    return lax.all_to_all(x, "seq", 0, 0, tiled=True)


def body(queries, keys, values, grad_out, lens, gain):
    width = queries.shape[2]
    n = width // HD
    half = n // 2
    gain = gain.reshape(n, 1, HD)
    unit = 2 * n * TOK * TOK * HD
    wide = struct((1, TOK, width), BF16)
    state_shape = (n * HD, HD)
    head_shape = (n, TOK, HD)
    slices = (N_SEQ, SLICE, HD)
    tok = lambda m, dtype=BF16: near((m, TOK, HD), dtype)
    sq = lambda m: near((m, HD, HD), BF16)
    column = lambda dtype: near((TOK, HD), dtype)
    square = near((TOK, HALF), BF16)
    mask_shape = struct((TOK, HALF), BF16)
    parts = 4
    scan_buf = near((parts, N_SEQ, SLICE // parts, HD), BF16)

    state, early = call(
        state_kernel, "state", [HBM] * 3, [HBM] * 2, [struct(state_shape, BF16)] * 2,
        [tok(n), tok(n), sq(n), sq(n), column(BF16)] + SCALARS + [sems(4, n)], unit // 4, 5 * MB,
    )(lens, keys, values)
    scattered = swap(state)
    local, mask, mask_t = call(
        attend_first_kernel, "attend_first", [HBM] * 4, [HBM] * 3,
        [struct(head_shape, LOCAL), mask_shape, mask_shape],
        [tok(half), tok(half), tok(half), tok(half, LOCAL), square, square] + SCALARS
        + [sems(2), sems(4, half)], unit, 6 * MB,
    )(lens, queries, keys, values)
    summed = call(
        scan_kernel, "scan", [ANY] * 2, ANY, struct(slices, BF16),
        [scan_buf, scan_buf] + SCALARS + [sems(2, parts)], MB, MB, grant=SMALL_GRANT,
    )(lens, scattered.reshape(slices))
    summed, local = lax.optimization_barrier((summed, local))
    carry_in = swap(summed).reshape(state_shape)
    local = call(
        attend_second_kernel, "attend_second", [HBM] * 5, HBM, struct(head_shape, LOCAL),
        [tok(half), tok(half), tok(half), tok(half, LOCAL), square, sems(), sems(4, half)],
        unit, 6 * MB, alias={4: 0},
    )(queries, keys, values, mask, local)
    sums = call(
        sums_kernel, "sums", [ANY] * 7, NEAR, struct((8, TOK), F32),
        [tok(n, LOCAL), tok(n), sq(n), sq(n), tok(n), near((n, 1, HD), F32), column(BF16),
         column(F32), column(F32)] + SCALARS + [sems(6, n)], unit // 4, 9 * MB, grant=PART_GRANT,
    )(lens, local, queries, carry_in, early, grad_out, gain)
    other = exchange(sums, "tensor")
    send_shape = (N_SEQ, SLICE + GG_ROWS, HD)
    layer_out, d_att, send, late = call(
        norm_kernel, "norm", [ANY] + [NEAR] * 2 + [ANY] * 5 + [NEAR], [ANY] * 4,
        [wide, struct(head_shape, BF16), struct(send_shape, BF16), struct(state_shape, BF16)],
        [tok(n, LOCAL), tok(n), sq(n), sq(n), tok(n), tok(n), tok(n), near(send_shape, BF16), sq(n),
         column(BF16), column(F32), column(F32), near((n, HD), F32)] + SCALARS + [sems(8, n)],
        unit // 2, 13 * MB, grant=PART_GRANT,
    )(lens, sums, other, local, queries, carry_in, early, grad_out, gain)
    back = swap(send)

    def gradients(first, count, *earlier):
        def kernel(*refs):
            grad_kernel(first, *refs[:9], *refs[9 + len(earlier):])

        return call(
            kernel, f"grad_from_{first}", [HBM] * (9 + len(earlier)), [HBM] * 3,
            [wide, struct(head_shape, LOCAL), struct(head_shape, LOCAL)],
            [tok(count)] * 4 + [sq(count), sq(count), tok(count), tok(count, LOCAL), tok(count, LOCAL),
                                square, square, column(BF16)] + SCALARS + [sems(2), sems(9, count)],
            4 * unit * count // n, 20 * MB * count // n,
            alias={9 + j: j for j in range(len(earlier))},
        )(lens, d_att, queries, keys, values, carry_in, early, mask, mask_t, *earlier)

    partial = gradients(0, BACK_SPLIT)
    gg_shape = (GG_ROWS // 2, HD)
    back_sum, gg_mine = call(
        scan_back_kernel, "scan_back", [ANY] * 2, [ANY, NEAR],
        [struct(slices, BF16), struct(gg_shape, F32)],
        [scan_buf, scan_buf, near((N_SEQ, GG_ROWS, HD), BF16)] + SCALARS + [sems(3, parts)], MB, MB,
        grant=SMALL_GRANT,
    )(lens, back)
    back_sum, gg_mine, *partial = lax.optimization_barrier((back_sum, gg_mine, *partial))
    carry_back = swap(back_sum).reshape(state_shape)
    gg_other = exchange(gg_mine, "dp")
    grad_queries, gk_local, gv_local = gradients(BACK_SPLIT, n - BACK_SPLIT, *partial)
    grad_keys, grad_values, grad_gain = call(
        close_kernel, "close", [ANY] * 7 + [NEAR] * 2, [ANY, ANY, NEAR],
        [wide, wide, struct(gg_shape, F32)],
        [tok(n, LOCAL), tok(n, LOCAL), tok(n), tok(n), sq(n), sq(n), tok(n), tok(n), column(BF16)]
        + SCALARS + [sems(8, n)], unit // 2, 17 * MB, grant=PART_GRANT,
    )(lens, gk_local, gv_local, keys, values, carry_back, late, gg_mine, gg_other)
    return layer_out, grad_queries, grad_keys, grad_values, grad_gain.reshape(width)


def solution(mesh):
    spread = P("dp", "seq", "tensor")
    return jax.shard_map(
        body, mesh=mesh,
        in_specs=(spread, spread, spread, spread, P("dp", None), P("tensor")),
        out_specs=(spread, spread, spread, spread, P("tensor")),
        check_vma=False,
    )
```
